32 devices in a mesh: ens: 8 (over z, x), row: 2 (over y), col: 2 (over core).
Axes of the slice: x: 2, y: 2, z: 4, core: 2. Of those that a mesh axis runs over, the one named last changes fastest.
Arguments:
- states: float32 [16, 16, 4096], P('ens', None, ('row', 'col')), parts along dimension 0, may hold values from -4 to 4
- jacobian: bfloat16 [32768, 4096], P(('ens', 'row'), 'col'), parts along dimension 0, as said below
- step_sizes: float32 [16, 1], P('ens'), parts along dimension 0, may hold values from 0.75 to 1.5
Outputs:
- new_states: float32 [16, 16, 4096], P('ens', None, ('row', 'col')), parts along dimension 0
The draws below stay inside these ranges and needn't reach their ends.
There are 8 independent parts, one for each index of `ens`. The reference program is written for one: setup_inputs(seed, part) draws one part's arguments, and reference() takes and returns one part's arrays. A program takes and returns all parts, laid end to end along the dimension named above; each array names one. Nothing has to cross between parts.
Inputs may be any that keep to these rules, and one draw needn't show every extreme that they name: `jacobian`: the diagonal lies between -40 and -1 apart from a term as small as the others, whose magnitude is at most 24 / sqrt(4096).
All inputs are finite; a program needn't handle non-finite values.
Results may differ from the reference program's by a relative error of at most 0.0083.
Values may be sent and summed in bfloat16 or wider, within the bound.
A program may use at most 64 MiB of HBM per device.

```python
import math
import jax
import jax.numpy as jnp
from jax import lax

N = 4096
COLS = 16
BLOCKS = 12
STEPS = 1
BATCH = 2


def draw_jacobian(key, part):
    first_key, second_key = jax.random.split(jax.random.fold_in(key, 11))
    spread = 4.0 / math.sqrt(N)
    rough = jnp.clip(jax.random.normal(first_key, (N, N), jnp.float32), -6.0, 6.0) * spread
    rates = jnp.exp(jax.random.uniform(second_key, (N,), jnp.float32, 0.0, math.log(40.0)))
    return (rough - jnp.diag(rates)).astype(jnp.bfloat16)


def block_scale(key, shape, pieces, low, top_value):
    loudness = 1.0
    for axis_at, parts in pieces:
        steps = jax.random.uniform(jax.random.fold_in(jax.random.fold_in(key, 6), axis_at), (parts,), jnp.float32, low / len(pieces), top_value / len(pieces))
        loudness = loudness * jnp.repeat(jnp.exp(steps), shape[axis_at] // parts).reshape((-1,) + (1,) * (len(shape) - 1 - axis_at))
    return loudness


def gaussian(stream_key, shape, scale, reach, shards=(), held_as=jnp.bfloat16):
    array = scale * jax.random.normal(stream_key, shape, jnp.float32)
    if shards:
        array = array * block_scale(stream_key, shape, shards, -0.22, 0.18)
    return jnp.clip(array, -reach, reach).astype(held_as)


def setup_inputs(seed: int = 0, part: int = 0) -> dict:
    keys = jax.random.split(jax.random.key(seed), 4)
    part_keys = jax.random.split(jax.random.fold_in(keys[3], part), 4)
    return {
        "states": gaussian(part_keys[0], (BATCH, COLS, N), 1.0, 4.0, ((2, 4),), jnp.float32),
        "jacobian": draw_jacobian(jax.random.fold_in(jax.random.fold_in(keys[3], part), 71), part),
        "step_sizes": jnp.clip(jnp.exp(jax.random.uniform(part_keys[2], (BATCH, STEPS), jnp.float32, math.log(0.75), math.log(1.5))), 0.75, 1.5),
    }


precise = lax.Precision.HIGHEST
squarings = 10
taylor_degree = 8

def exponential(matrix):
    scaled = matrix / 2.0 ** squarings
    identity = jnp.eye(matrix.shape[-1], dtype=jnp.float32)
    result = jnp.broadcast_to(identity, matrix.shape)
    for degree in range(taylor_degree, 0, -1):
        result = identity + jnp.matmul(scaled, result, precision=precise) / degree
    for squaring in range(squarings):
        result = jnp.matmul(result, result, precision=precise)
    return result

def apply_full(vectors, matrix):
    rounded = lax.optimization_barrier(vectors.astype(jnp.bfloat16)).astype(jnp.float32)
    return jnp.einsum('bcm,nm->bcn', rounded, matrix, precision=precise)

def reference(states, jacobian, step_sizes):
    matrix = jacobian.astype(jnp.float32)
    members = states.shape[0]
    columns = states.shape[1]
    length = states.shape[2]
    krylov = BLOCKS * columns
    for step_index in range(STEPS):
        forcing = apply_full(states, matrix) - states * states * states / 3.0
        root_gram = jnp.einsum('bpn,bqn->bpq', forcing, forcing, precision=precise)
        root_lower = jnp.linalg.cholesky(root_gram)
        leading = lax.linalg.triangular_solve(root_lower, forcing, left_side=True, lower=True)
        krylov_basis = jnp.zeros((members, krylov, length), jnp.float32).at[:, :columns].set(leading)
        hessenberg = jnp.zeros((members, krylov, krylov), jnp.float32)
        for block_index in range(BLOCKS):
            start = block_index * columns
            current = krylov_basis[:, start:start + columns]
            images = apply_full(current, matrix)
            projection = jnp.einsum('bkn,bqn->bkq', krylov_basis, images, precision=precise)
            hessenberg = hessenberg.at[:, :, start:start + columns].set(projection)
            if block_index + 1 < BLOCKS:
                reduced = images - jnp.einsum('bkq,bkn->bqn', projection, krylov_basis, precision=precise)
                gram_matrix = jnp.einsum('bpn,bqn->bpq', reduced, reduced, precision=precise)
                lower_factor = jnp.linalg.cholesky(gram_matrix)
                next_block = lax.linalg.triangular_solve(lower_factor, reduced, left_side=True, lower=True)
                hessenberg = hessenberg.at[:, start + columns:start + 2 * columns, start:start + columns].set(jnp.swapaxes(lower_factor, 1, 2))
                krylov_basis = krylov_basis.at[:, start + columns:start + 2 * columns].set(next_block)
        step_size = step_sizes[:, step_index][:, None, None]
        augmented = jnp.zeros((members, krylov + columns, krylov + columns), jnp.float32)
        augmented = augmented.at[:, :krylov, :krylov].set(step_size * hessenberg)
        augmented = augmented.at[:, :columns, krylov:].set(step_size * jnp.swapaxes(root_lower, 1, 2))
        exponent = exponential(augmented)
        phi_block = exponent[:, :krylov, krylov:]
        states = states + jnp.einsum('bkq,bkn->bqn', phi_block, krylov_basis, precision=precise)
    return states
```

```python
import functools

import jax
import jax.numpy as jnp
from jax import lax
from jax.experimental import pallas as pl
from jax.experimental.pallas import tpu as pltpu
from jax.sharding import PartitionSpec as P

BLOCKS = 12
SQUARINGS = 10
MESH = pl.DeviceIdType.MESH
NN = (((1,), (0,)), ((), ()))
NT = (((1,), (1,)), ((), ()))
f32, bf16 = jnp.float32, jnp.bfloat16
precise = lax.Precision.HIGHEST


def split(value):
    high = value.astype(bf16)
    return high, (value - high.astype(f32)).astype(bf16)


def product(left, right, dims):
    rows = left[0].shape[0]
    both = jnp.concatenate(left, axis=0)
    wide = lax.dot_general(both, right[0], dims, preferred_element_type=f32)
    low = lax.dot_general(left[0], right[1], dims, preferred_element_type=f32)
    return wide[:rows] + (wide[rows:] + low)


def factor(gram, place, offset):
    columns = gram.shape[0]
    sub = lax.broadcasted_iota(jnp.int32, (columns, 1), 0)
    lanes_inv = lax.broadcasted_iota(jnp.int32, (columns, place[1]), 1)
    inverse = jnp.where(lanes_inv == sub + place[0], 1.0, 0.0).astype(f32)
    lanes = lax.broadcasted_iota(jnp.int32, (columns, offset[1]), 1)
    lower = jnp.zeros((columns, offset[1]), f32)
    for k in range(columns):
        pivot = gram[k : k + 1, k : k + 1]
        root = lax.rsqrt(pivot)
        root = root * (1.5 - 0.5 * pivot * root * root)
        column = gram[:, k : k + 1] * root
        column = jnp.where(sub >= k, column, 0.0)
        lower = jnp.where(lanes == offset[0] + k, column, lower)
        below = jnp.where(sub > k, column, 0.0)
        row = gram[k : k + 1, :] * root
        row_inv = inverse[k : k + 1, :] * root
        gram = gram - below * row
        inverse = jnp.where(sub == k, row_inv, inverse - below * row_inv)
    return inverse, lower


def kernel(
    nr, nc, states_ref, jac_hbm, steps_ref, out_ref,
    jac, own, gathered, part_send, part_recv, high, low, w_ref, sums, aug,
    jac_sem, g_send, g_recv, p_send, p_recv, s_send, s_recv,
):
    members, columns, length = states_ref.shape
    stacked = members * columns
    width = high.shape[1]
    r, c = lax.axis_index("row"), lax.axis_index("col")
    me = r * nc + c
    count = nr * nc

    load = pltpu.make_async_copy(jac_hbm, jac, jac_sem)
    load.start()
    barrier = pltpu.get_barrier_semaphore()
    for step in range(1, count):
        peer = lax.rem(me + step, count)
        pl.semaphore_signal(
            barrier, inc=1, device_id={"row": peer // nc, "col": lax.rem(peer, nc)},
            device_id_type=MESH,
        )
    high[...] = jnp.zeros_like(high)
    low[...] = jnp.zeros_like(low)
    aug[...] = jnp.zeros_like(aug)
    own[...] = states_ref[...].reshape(stacked, length).astype(bf16)
    pl.semaphore_wait(barrier, count - 1)

    def block_copy(target):
        return pltpu.make_async_remote_copy(
            src_ref=own, dst_ref=gathered.at[c], send_sem=g_send.at[target],
            recv_sem=g_recv.at[c], device_id={"row": target, "col": r}, device_id_type=MESH,
        )

    def block_arrival(source):
        return pltpu.make_async_remote_copy(
            src_ref=own, dst_ref=gathered.at[source], send_sem=g_send.at[0],
            recv_sem=g_recv.at[source], device_id={"row": c, "col": source}, device_id_type=MESH,
        )

    def sum_copy(slot, step):
        peer = lax.rem(me + step, count)
        return pltpu.make_async_remote_copy(
            src_ref=sums.at[slot, me], dst_ref=sums.at[slot, me], send_sem=s_send.at[step - 1],
            recv_sem=s_recv.at[slot, me],
            device_id={"row": peer // nc, "col": lax.rem(peer, nc)}, device_id_type=MESH,
        )

    def sum_arrival(slot, step):
        peer = lax.rem(me + step, count)
        return pltpu.make_async_remote_copy(
            src_ref=sums.at[slot, peer], dst_ref=sums.at[slot, peer], send_sem=s_send.at[step - 1],
            recv_sem=s_recv.at[slot, peer],
            device_id={"row": peer // nc, "col": lax.rem(peer, nc)}, device_id_type=MESH,
        )

    def piece(owner):
        rows = pl.ds(pl.multiple_of(owner * length, length), length)
        total = None
        for source in range(nr):
            term = lax.dot_general(
                gathered[source], jac[rows, source * length : (source + 1) * length], NT,
                preferred_element_type=f32,
            )
            total = term if total is None else total + term
        return total

    def turn(t, carry):
        for target in range(nr):
            @pl.when(jnp.logical_and(target == r, c == r))
            def _():
                gathered[c] = own[...]

            @pl.when(jnp.logical_not(jnp.logical_and(target == r, c == r)))
            def _():
                block_copy(target).start()

        @pl.when(t == 0)
        def _():
            load.wait()

        for source in range(nc):
            @pl.when(jnp.logical_not(jnp.logical_and(c == r, source == c)))
            def _():
                block_arrival(source).wait_recv()

        other = 1 - c
        part_send[...] = piece(other)
        partial = pltpu.make_async_remote_copy(
            src_ref=part_send, dst_ref=part_recv, send_sem=p_send, recv_sem=p_recv,
            device_id={"row": r, "col": other}, device_id_type=MESH,
        )
        partial.start()
        w_ref[...] = piece(c)
        for target in range(nr):
            @pl.when(jnp.logical_not(jnp.logical_and(target == r, c == r)))
            def _():
                block_copy(target).wait_send()
        partial.wait()
        w_ref[...] = w_ref[...] + part_recv[...]

        @pl.when(t == 0)
        def _():
            first = states_ref[...].reshape(stacked, length)
            w_ref[...] = w_ref[...] - first * first * first / 3.0

        slot = lax.rem(t, 2)
        for b in range(members):
            w_high, w_low = split(w_ref[b * columns : (b + 1) * columns, :])
            high[b, :columns, :] = w_high
            low[b, :columns, :] = w_low
            sums[slot, me, b * columns : (b + 1) * columns, :] = product(
                (w_high, w_low), (high[b], low[b]), NT
            )
        for step in range(1, count):
            sum_copy(slot, step).start()
        for step in range(1, count):
            sum_arrival(slot, step).wait_recv()
        total = sums[slot, 0]
        for index in range(1, count):
            total = total + sums[slot, index]
        for step in range(1, count):
            sum_copy(slot, step).wait_send()

        lanes = lax.broadcasted_iota(jnp.int32, (stacked, width), 1)
        projection = jnp.where(lanes >= columns, total, 0.0)
        start = pl.multiple_of(t * columns, columns)

        @pl.when(t == BLOCKS)
        def _():
            for b in range(members):
                aug[b, pl.ds(start, columns), :] = projection[b * columns : (b + 1) * columns]

        @pl.when(t < BLOCKS)
        def _():
            inverses, reduced = [], []
            for b in range(members):
                rows = slice(b * columns, (b + 1) * columns)
                mine = projection[rows]
                gram = total[rows, :columns] - lax.dot_general(
                    mine, mine, NT, precision=precise, preferred_element_type=f32
                )
                inverse, lower = factor(
                    gram, (b * columns, stacked), ((t + 1) * columns, width)
                )
                aug[b, pl.ds(start, columns), :] = mine + lower
                inverses.append(inverse)
                reduced.append(w_ref[rows, :] - product(split(mine), (high[b], low[b]), NN))
            following = lax.dot_general(
                jnp.concatenate(inverses, axis=0), jnp.concatenate(reduced, axis=0), NN,
                precision=precise, preferred_element_type=f32,
            )
            next_high, next_low = split(following)
            own[...] = next_high
            after = pl.multiple_of((t + 1) * columns, columns)
            for b in range(members):
                rows = slice(b * columns, (b + 1) * columns)
                high[b, pl.ds(after, columns), :] = next_high[rows]
                low[b, pl.ds(after, columns), :] = next_low[rows]

        return carry

    lax.fori_loop(0, BLOCKS + 1, turn, 0)

    for b in range(members):
        x = aug[b] * (steps_ref[b, 0] / 2.0**SQUARINGS)
        xs = split(x)
        x2 = product(xs, xs, NN)
        x2s = split(x2)
        x3 = product(xs, x2s, NN)
        x4 = product(x2s, x2s, NN)
        tail = x / 120.0 + x2 / 720.0 + x3 / 5040.0 + x4 / 40320.0
        aug[b] = x + x2 / 2.0 + x3 / 6.0 + x4 / 24.0 + product(split(x4), split(tail), NN)

    def square(index, carry):
        for b in range(members):
            now = aug[b]
            pair = split(now)
            aug[b] = 2.0 * now + product(pair, pair, NN)
        return carry

    lax.fori_loop(0, SQUARINGS - 1, square, 0)
    for b in range(members):
        now = aug[b]
        top = now[:columns]
        phi = 2.0 * top + product(split(top), split(now), NN)
        out_ref[b] = states_ref[b] + product(split(phi), (high[b], low[b]), NN)


def local(nr, nc, states, jacobian, step_sizes):
    members, columns, length = states.shape
    stacked = members * columns
    width = -(-(BLOCKS + 1) * columns // 128) * 128
    vmem = pl.BlockSpec(memory_space=pltpu.VMEM)
    dma = pltpu.SemaphoreType.DMA
    return pl.pallas_call(
        functools.partial(kernel, nr, nc),
        out_shape=jax.ShapeDtypeStruct(states.shape, f32),
        in_specs=[vmem, pl.BlockSpec(memory_space=pl.ANY), pl.BlockSpec(memory_space=pltpu.SMEM)],
        out_specs=vmem,
        scratch_shapes=[
            pltpu.VMEM(jacobian.shape, bf16),
            pltpu.VMEM((stacked, length), bf16),
            pltpu.VMEM((nr, stacked, length), bf16),
            pltpu.VMEM((stacked, length), f32),
            pltpu.VMEM((stacked, length), f32),
            pltpu.VMEM((members, width, length), bf16),
            pltpu.VMEM((members, width, length), bf16),
            pltpu.VMEM((stacked, length), f32),
            pltpu.VMEM((2, nr * nc, stacked, width), f32),
            pltpu.VMEM((members, width, width), f32),
            dma, dma((nr,)), dma((nr,)), dma, dma, dma((nr * nc - 1,)), dma((2, nr * nc)),
        ],
        compiler_params=pltpu.CompilerParams(
            collective_id=0, has_side_effects=True, vmem_limit_bytes=48 * 2**20
        ),
    )(states, jacobian, step_sizes)


def solution(mesh):
    placed = (P("ens", None, ("row", "col")), P(("ens", "row"), "col"), P("ens", None))
    return jax.shard_map(
        functools.partial(local, mesh.shape["row"], mesh.shape["col"]), mesh=mesh,
        in_specs=placed, out_specs=P("ens", None, ("row", "col")), check_vma=False,
    )
```

```python
import functools

import jax
import jax.numpy as jnp
from jax import lax
from jax.experimental import pallas as pl
from jax.experimental.pallas import tpu as pltpu
from jax.sharding import PartitionSpec as P

BLOCKS = 12
SQUARINGS = 10
CHUNKS = 4
LANES = 128
PIECES = 2
MESH = pl.DeviceIdType.MESH
NN = (((1,), (0,)), ((), ()))
NT = (((1,), (1,)), ((), ()))
f32, bf16 = jnp.float32, jnp.bfloat16
precise = lax.Precision.HIGHEST


def split(value):
    high = value.astype(bf16)
    return high, (value - high.astype(f32)).astype(bf16)


def product(left, right, dims):
    rows = left[0].shape[0]
    both = jnp.concatenate(left, axis=0)
    wide = lax.dot_general(both, right[0], dims, preferred_element_type=f32)
    low = lax.dot_general(left[0], right[1], dims, preferred_element_type=f32)
    return wide[:rows] + (wide[rows:] + low)


def factor(block, offset, width):
    columns, lanes_all = block.shape
    sub = lax.broadcasted_iota(jnp.int32, block.shape, 0)
    lanes = lax.broadcasted_iota(jnp.int32, block.shape, 1)
    lower = [jnp.zeros(block.shape, f32) for _ in range(width // lanes_all)]
    for k in range(columns):
        column = jnp.broadcast_to(block[:, k : k + 1], block.shape)
        pivot = column[k : k + 1, :]
        root = lax.rsqrt(pivot)
        root = root * (1.5 - 0.5 * pivot * root * root)
        column = jnp.where(sub >= k, column * root, 0.0)
        row = block[k : k + 1, :] * root
        block = jnp.where(sub == k, row, block - column * row)
        lower = [
            jnp.where(lanes == offset + k - i * lanes_all, column, part)
            for i, part in enumerate(lower)
        ]
    return block[:, columns : 2 * columns], jnp.concatenate(lower, axis=1)


def kernel(
    nr, nc, states_ref, jac_hbm, steps_ref, out_ref,
    jac, own, gathered, acc, part_recv, high, low, w_ref, sums, aug, start_states, last,
    jac_sem, g_send, g_recv, p_send, p_recv, s_send, s_recv, e_send, e_recv,
):
    length = states_ref.shape[1]
    per, width, cells = high.shape
    mine = w_ref.shape[0]
    columns = mine // per
    piece = cells // PIECES
    chunk = cells // CHUNKS
    r, c = lax.axis_index("row"), lax.axis_index("col")
    other = 1 - c
    to_self = c == r

    load = pltpu.make_async_copy(jac_hbm, jac, jac_sem)
    load.start()
    barrier = pltpu.get_barrier_semaphore()
    for row in range(nr):
        for col in range(nc):
            @pl.when(jnp.logical_not(jnp.logical_and(r == row, c == col)))
            def _():
                pl.semaphore_signal(
                    barrier, inc=1, device_id={"row": row, "col": col}, device_id_type=MESH
                )
    my_rows = pl.ds(pl.multiple_of(c * mine, mine), mine)
    other_rows = pl.ds(pl.multiple_of(other * mine, mine), mine)
    my_cells = pl.ds(pl.multiple_of(c * length, length), length)
    other_cells = pl.ds(pl.multiple_of(other * length, length), length)
    high[...] = jnp.zeros_like(high)
    low[...] = jnp.zeros_like(low)
    aug[...] = jnp.zeros_like(aug)
    start_states[:, my_cells] = states_ref[my_rows, :]
    pl.semaphore_wait(barrier, nr * nc - 1)

    def block_copy(target, k):
        return pltpu.make_async_remote_copy(
            src_ref=own.at[k], dst_ref=gathered.at[k, my_rows], send_sem=g_send.at[target, k],
            recv_sem=g_recv.at[c, k], device_id={"row": target, "col": r}, device_id_type=MESH,
        )

    def block_arrival(source, k):
        return pltpu.make_async_remote_copy(
            src_ref=own.at[k], dst_ref=gathered.at[k, source * mine : (source + 1) * mine],
            send_sem=g_send.at[0, k], recv_sem=g_recv.at[source, k],
            device_id={"row": c, "col": source}, device_id_type=MESH,
        )

    def send_block(k):
        @pl.when(to_self)
        def _():
            gathered[k, my_rows, :] = own[k]

        for target in range(nr):
            @pl.when(jnp.logical_not(jnp.logical_and(target == r, to_self)))
            def _():
                block_copy(target, k).start()

    def sum_copy(slot, step):
        return pltpu.make_async_remote_copy(
            src_ref=sums.at[slot, r], dst_ref=sums.at[slot, r], send_sem=s_send.at[step - 1],
            recv_sem=s_recv.at[slot, r],
            device_id={"row": lax.rem(r + step, nr), "col": c}, device_id_type=MESH,
        )

    def sum_arrival(slot, step):
        peer = lax.rem(r + step, nr)
        return pltpu.make_async_remote_copy(
            src_ref=sums.at[slot, peer], dst_ref=sums.at[slot, peer], send_sem=s_send.at[step - 1],
            recv_sem=s_recv.at[slot, peer],
            device_id={"row": peer, "col": c}, device_id_type=MESH,
        )

    def exchange(source, target, index):
        return pltpu.make_async_remote_copy(
            src_ref=source, dst_ref=target, send_sem=e_send.at[index], recv_sem=e_recv.at[index],
            device_id={"row": r, "col": other}, device_id_type=MESH,
        )

    first = exchange(states_ref.at[other_rows], start_states.at[:, my_cells], 0)
    first.start()
    first.wait_send()
    exchange(states_ref.at[other_rows], start_states.at[:, other_cells], 0).wait_recv()
    for k in range(CHUNKS):
        own[k] = start_states[:, k * chunk : (k + 1) * chunk].astype(bf16)
        send_block(k)

    def turn(t, carry):
        @pl.when(t == 0)
        def _():
            load.wait()

        partials = []
        for k in range(CHUNKS):
            for source in range(nc):
                @pl.when(jnp.logical_not(jnp.logical_and(to_self, source == c)))
                def _():
                    block_arrival(source, k).wait_recv()

            for i in range(PIECES):
                rows = slice(i * piece, (i + 1) * piece)
                term = lax.dot_general(
                    gathered[k], jac[rows, k * chunk : (k + 1) * chunk], NT,
                    preferred_element_type=f32,
                )
                acc[:, rows] = term if k == 0 else acc[:, rows] + term
                if k == CHUNKS - 1:
                    partial = pltpu.make_async_remote_copy(
                        src_ref=acc.at[other_rows, rows], dst_ref=part_recv.at[:, rows],
                        send_sem=p_send.at[i], recv_sem=p_recv.at[i],
                        device_id={"row": r, "col": other}, device_id_type=MESH,
                    )
                    partial.start()
                    partials.append(partial)
        for k in range(CHUNKS):
            for target in range(nr):
                @pl.when(jnp.logical_not(jnp.logical_and(target == r, to_self)))
                def _():
                    block_copy(target, k).wait_send()
        for partial in partials:
            partial.wait()
        w_ref[...] = acc[my_rows, :] + part_recv[...]

        @pl.when(t == 0)
        def _():
            first = start_states[...]
            w_ref[...] = w_ref[...] - first * first * first / 3.0

        slot = lax.rem(t, 2)
        for b in range(per):
            rows = slice(b * columns, (b + 1) * columns)
            w_high, w_low = split(w_ref[rows, :])
            high[b, :columns, :] = w_high
            low[b, :columns, :] = w_low
            sums[slot, r, rows, :] = product((w_high, w_low), (high[b], low[b]), NT)
        for step in range(1, nr):
            sum_copy(slot, step).start()
        for step in range(1, nr):
            sum_arrival(slot, step).wait_recv()
        total = sums[slot, 0]
        for index in range(1, nr):
            total = total + sums[slot, index]
        for step in range(1, nr):
            sum_copy(slot, step).wait_send()

        lanes = lax.broadcasted_iota(jnp.int32, (mine, width), 1)
        projection = jnp.where(lanes >= columns, total, 0.0)
        start = pl.multiple_of(t * columns, columns)

        @pl.when(t == BLOCKS)
        def _():
            for b in range(per):
                aug[b, pl.ds(start, columns), :] = projection[b * columns : (b + 1) * columns]

        @pl.when(t < BLOCKS)
        def _():
            inverses, pairs = [], []
            for b in range(per):
                rows = slice(b * columns, (b + 1) * columns)
                term = projection[rows]
                padded = jnp.concatenate([term, jnp.zeros((LANES - columns, width), f32)], axis=0)
                gram = total[rows, :LANES] - lax.dot_general(
                    term, padded, NT, precision=precise, preferred_element_type=f32
                )
                sub = lax.broadcasted_iota(jnp.int32, (columns, LANES), 0)
                lane = lax.broadcasted_iota(jnp.int32, (columns, LANES), 1)
                unit = jnp.where(lane == sub + columns, 1.0, 0.0)
                block = jnp.where(lane < columns, gram, unit)
                inverse, lower = factor(block, (t + 1) * columns, width)
                aug[b, pl.ds(start, columns), :] = term + lower
                inverses.append(split(inverse))
                pairs.append(split(term))
            after = pl.multiple_of((t + 1) * columns, columns)
            for k in range(CHUNKS):
                at = slice(k * chunk, (k + 1) * chunk)
                for b in range(per):
                    rows = slice(b * columns, (b + 1) * columns)
                    reduced = w_ref[rows, at] - product(
                        pairs[b], (high[b, :, at], low[b, :, at]), NN
                    )
                    next_high, next_low = split(product(inverses[b], split(reduced), NN))
                    own[k, rows, :] = next_high
                    high[b, pl.ds(after, columns), at] = next_high
                    low[b, pl.ds(after, columns), at] = next_low
                send_block(k)

        return carry

    lax.fori_loop(0, BLOCKS + 1, turn, 0)

    for b in range(per):
        x = aug[b] * (steps_ref[c * per + b, 0] / 2.0**SQUARINGS)
        xs = split(x)
        x2 = product(xs, xs, NN)
        x2s = split(x2)
        x3 = product(xs, x2s, NN)
        x4 = product(x2s, x2s, NN)
        tail = x / 120.0 + x2 / 720.0 + x3 / 5040.0 + x4 / 40320.0
        aug[b] = x + x2 / 2.0 + x3 / 6.0 + x4 / 24.0 + product(split(x4), split(tail), NN)

    def square(index, carry):
        for b in range(per):
            now = aug[b]
            pair = split(now)
            aug[b] = 2.0 * now + product(pair, pair, NN)
        return carry

    lax.fori_loop(0, SQUARINGS - 1, square, 0)
    for b in range(per):
        rows = slice(b * columns, (b + 1) * columns)
        now = aug[b]
        top = now[:columns]
        phi = 2.0 * top + product(split(top), split(now), NN)
        w_ref[rows, :] = start_states[rows, :] + product(split(phi), (high[b], low[b]), NN)
    final = exchange(w_ref.at[:, other_cells], last, 1)
    final.start()
    out_ref[my_rows, :] = w_ref[:, my_cells]
    final.wait()
    out_ref[other_rows, :] = last[...]


def local(nr, nc, states, jacobian, step_sizes):
    members, columns, length = states.shape
    stacked = members * columns
    per = members // nc
    mine = per * columns
    cells = nc * length
    assert nr == nc == 2 and per * nc == members and jacobian.shape == (cells, cells)
    width = -(-(BLOCKS + 1) * columns // LANES) * LANES
    vmem = pl.BlockSpec(memory_space=pltpu.VMEM)
    dma = pltpu.SemaphoreType.DMA
    out = pl.pallas_call(
        functools.partial(kernel, nr, nc),
        out_shape=jax.ShapeDtypeStruct((stacked, length), f32),
        in_specs=[vmem, pl.BlockSpec(memory_space=pl.ANY), pl.BlockSpec(memory_space=pltpu.SMEM)],
        out_specs=vmem,
        scratch_shapes=[
            pltpu.VMEM(jacobian.shape, bf16),
            pltpu.VMEM((CHUNKS, mine, cells // CHUNKS), bf16),
            pltpu.VMEM((CHUNKS, stacked, cells // CHUNKS), bf16),
            pltpu.VMEM((stacked, cells), f32),
            pltpu.VMEM((mine, cells), f32),
            pltpu.VMEM((per, width, cells), bf16),
            pltpu.VMEM((per, width, cells), bf16),
            pltpu.VMEM((mine, cells), f32),
            pltpu.VMEM((2, nr, mine, width), f32),
            pltpu.VMEM((per, width, width), f32),
            pltpu.VMEM((mine, cells), f32),
            pltpu.VMEM((mine, length), f32),
            dma, dma((nr, CHUNKS)), dma((nc, CHUNKS)), dma((PIECES,)), dma((PIECES,)),
            dma((nr - 1,)), dma((2, nr)), dma((2,)), dma((2,)),
        ],
        compiler_params=pltpu.CompilerParams(
            collective_id=0, has_side_effects=True, vmem_limit_bytes=48 * 2**20
        ),
    )(states.reshape(stacked, length), jacobian, step_sizes)
    return out.reshape(states.shape)


def solution(mesh):
    placed = (P("ens", None, ("row", "col")), P(("ens", "row"), "col"), P("ens", None))
    return jax.shard_map(
        functools.partial(local, mesh.shape["row"], mesh.shape["col"]), mesh=mesh,
        in_specs=placed, out_specs=P("ens", None, ("row", "col")), check_vma=False,
    )
```

```python
import functools

import jax
import jax.numpy as jnp
from jax import lax
from jax.experimental import pallas as pl
from jax.experimental.pallas import tpu as pltpu
from jax.sharding import PartitionSpec as P

BLOCKS = 12
SQUARINGS = 10
CHUNKS = 2
GROUP = 4
LANES = 128
MESH = pl.DeviceIdType.MESH
NN = (((1,), (0,)), ((), ()))
NT = (((1,), (1,)), ((), ()))
f32, bf16 = jnp.float32, jnp.bfloat16


def split(value):
    high = value.astype(bf16)
    return high, (value - high.astype(f32)).astype(bf16)


def product(left, right, dims):
    rows = left[0].shape[0]
    both = jnp.concatenate(left, axis=0)
    wide = lax.dot_general(both, right[0], dims, preferred_element_type=f32)
    low = lax.dot_general(left[0], right[1], dims, preferred_element_type=f32)
    return wide[:rows] + (wide[rows:] + low)


def factor(gram, place, offset):
    columns = gram.shape[0]
    lanes_inv = lax.broadcasted_iota(jnp.int32, (columns, place[1]), 1)
    diagonal = lax.broadcasted_iota(jnp.int32, (columns, place[1]), 0) + place[0]
    inverse = jnp.where(lanes_inv == diagonal, 1.0, 0.0).astype(f32)
    lanes = lax.broadcasted_iota(jnp.int32, (columns, offset[1]), 1)
    lower = jnp.zeros((columns, offset[1]), f32)
    sub = lax.broadcasted_iota(jnp.int32, (columns, LANES), 0)
    sub_inv = lax.broadcasted_iota(jnp.int32, (columns, place[1]), 0)
    for base in range(0, columns, GROUP):
        held = [
            jnp.broadcast_to(gram[:, base + i : base + i + 1], (columns, LANES))
            for i in range(GROUP)
        ]
        for i in range(GROUP):
            k = base + i
            pivot = held[i][k : k + 1, :]
            root = lax.rsqrt(pivot)
            root = root * (1.5 - 0.5 * pivot * root * root)
            column = jnp.where(sub >= k, held[i] * root, 0.0)
            below = jnp.where(sub > k, column, 0.0)
            for later in range(i + 1, GROUP):
                index = base + later
                held[later] = held[later] - below * column[index : index + 1, :]
            wide = jnp.concatenate([column] * (offset[1] // LANES), axis=1)
            lower = jnp.where(lanes == offset[0] + k, wide, lower)
            row = gram[k : k + 1, :] * root[:, :columns]
            row_inv = inverse[k : k + 1, :] * root[:, : place[1]]
            gram = gram - below[:, :columns] * row
            inverse = jnp.where(sub_inv == k, row_inv, inverse - below[:, : place[1]] * row_inv)
    return inverse, lower


def kernel(
    nr, nc, states_ref, jac_hbm, steps_ref, out_ref,
    jac, own, gathered, part_send, part_recv, high, low, w_ref, sums, aug,
    jac_sem, g_send, g_recv, p_send, p_recv, s_send, s_recv,
):
    members, columns, length = states_ref.shape
    stacked = members * columns
    width = high.shape[1]
    tiles = width // LANES
    chunk = length // CHUNKS
    r, c = lax.axis_index("row"), lax.axis_index("col")
    me = r * nc + c
    count = nr * nc

    load = pltpu.make_async_copy(jac_hbm, jac, jac_sem)
    load.start()
    barrier = pltpu.get_barrier_semaphore()
    for step in range(1, count):
        peer = lax.rem(me + step, count)
        pl.semaphore_signal(
            barrier, inc=1, device_id={"row": peer // nc, "col": lax.rem(peer, nc)},
            device_id_type=MESH,
        )
    high[...] = jnp.zeros_like(high)
    low[...] = jnp.zeros_like(low)
    aug[...] = jnp.zeros_like(aug)
    sums[...] = jnp.zeros_like(sums)
    pl.semaphore_wait(barrier, count - 1)

    to_self = c == r

    def block_copy(target, k):
        return pltpu.make_async_remote_copy(
            src_ref=own.at[k], dst_ref=gathered.at[c, k], send_sem=g_send.at[target, k],
            recv_sem=g_recv.at[c, k], device_id={"row": target, "col": r}, device_id_type=MESH,
        )

    def block_arrival(source, k):
        return pltpu.make_async_remote_copy(
            src_ref=own.at[k], dst_ref=gathered.at[source, k], send_sem=g_send.at[0, k],
            recv_sem=g_recv.at[source, k], device_id={"row": c, "col": source}, device_id_type=MESH,
        )

    def send_block(k):
        for target in range(nr):
            @pl.when(jnp.logical_not(jnp.logical_and(target == r, to_self)))
            def _():
                block_copy(target, k).start()

        @pl.when(to_self)
        def _():
            gathered[c, k] = own[k]

    def sum_copy(slot, step, i):
        peer = lax.rem(me + step, count)
        return pltpu.make_async_remote_copy(
            src_ref=sums.at[slot, me, i], dst_ref=sums.at[slot, me, i],
            send_sem=s_send.at[step - 1, i], recv_sem=s_recv.at[slot, me, i],
            device_id={"row": peer // nc, "col": lax.rem(peer, nc)}, device_id_type=MESH,
        )

    def sum_arrival(slot, step, i):
        peer = lax.rem(me + step, count)
        return pltpu.make_async_remote_copy(
            src_ref=sums.at[slot, peer, i], dst_ref=sums.at[slot, peer, i],
            send_sem=s_send.at[step - 1, i], recv_sem=s_recv.at[slot, peer, i],
            device_id={"row": peer // nc, "col": lax.rem(peer, nc)}, device_id_type=MESH,
        )

    def piece(owner, arrive):
        rows = pl.ds(pl.multiple_of(owner * length, length), length)
        total = None
        for k in range(CHUNKS):
            for source in range(nc):
                if arrive:
                    @pl.when(jnp.logical_not(jnp.logical_and(to_self, source == c)))
                    def _():
                        block_arrival(source, k).wait_recv()

                first = source * length + k * chunk
                term = lax.dot_general(
                    gathered[source, k], jac[rows, first : first + chunk], NT,
                    preferred_element_type=f32,
                )
                total = term if total is None else total + term
        return total

    for k in range(CHUNKS):
        own[k] = states_ref[...].reshape(stacked, length)[:, k * chunk : (k + 1) * chunk].astype(bf16)
        send_block(k)

    def turn(t, carry):
        @pl.when(t == 0)
        def _():
            load.wait()

        other = 1 - c
        part_send[...] = piece(other, True)
        partial = pltpu.make_async_remote_copy(
            src_ref=part_send, dst_ref=part_recv, send_sem=p_send, recv_sem=p_recv,
            device_id={"row": r, "col": other}, device_id_type=MESH,
        )
        partial.start()
        w_ref[...] = piece(c, False)
        for k in range(CHUNKS):
            for target in range(nr):
                @pl.when(jnp.logical_not(jnp.logical_and(target == r, to_self)))
                def _():
                    block_copy(target, k).wait_send()
        partial.wait()
        w_ref[...] = w_ref[...] + part_recv[...]

        @pl.when(t == 0)
        def _():
            first = states_ref[...].reshape(stacked, length)
            w_ref[...] = w_ref[...] - first * first * first / 3.0

        slot = lax.rem(t, 2)
        halves = []
        for b in range(members):
            w_high, w_low = split(w_ref[b * columns : (b + 1) * columns, :])
            high[b, :columns, :] = w_high
            low[b, :columns, :] = w_low
            halves.append((w_high, w_low))

        def project(i):
            at = slice(i * LANES, (i + 1) * LANES)
            for b in range(members):
                sums[slot, me, i, b * columns : (b + 1) * columns, :] = product(
                    halves[b], (high[b, at], low[b, at]), NT
                )
            for step in range(1, count):
                sum_copy(slot, step, i).start()

        def collect(i):
            for step in range(1, count):
                sum_arrival(slot, step, i).wait_recv()
            for step in range(1, count):
                sum_copy(slot, step, i).wait_send()

        project(0)
        for i in range(1, tiles):
            pl.when((t + 1) * columns > i * LANES)(functools.partial(project, i))
        collect(0)
        for i in range(1, tiles):
            pl.when((t + 1) * columns > i * LANES)(functools.partial(collect, i))
        parts = []
        for i in range(tiles):
            part = sums[slot, 0, i]
            for index in range(1, count):
                part = part + sums[slot, index, i]
            parts.append(part)
        total = jnp.concatenate(parts, axis=1)

        lanes = lax.broadcasted_iota(jnp.int32, (stacked, width), 1)
        projection = jnp.where(lanes >= columns, total, 0.0)
        start = pl.multiple_of(t * columns, columns)

        @pl.when(t == BLOCKS)
        def _():
            for b in range(members):
                aug[b, pl.ds(start, columns), :] = projection[b * columns : (b + 1) * columns]

        @pl.when(t < BLOCKS)
        def _():
            inverses, pairs = [], []
            for b in range(members):
                rows = slice(b * columns, (b + 1) * columns)
                term = projection[rows]
                pair = split(term)
                gram = total[rows, :columns] - product(pair, pair, NT)
                inverse, lower = factor(
                    gram, (b * columns, stacked), ((t + 1) * columns, width)
                )
                aug[b, pl.ds(start, columns), :] = term + lower
                inverses.append(inverse)
                pairs.append(pair)
            inverse = split(jnp.concatenate(inverses, axis=0))
            after = pl.multiple_of((t + 1) * columns, columns)
            for k in range(CHUNKS):
                at = slice(k * chunk, (k + 1) * chunk)
                reduced = jnp.concatenate(
                    [
                        w_ref[b * columns : (b + 1) * columns, at]
                        - product(pairs[b], (high[b, :, at], low[b, :, at]), NN)
                        for b in range(members)
                    ],
                    axis=0,
                )
                next_high, next_low = split(product(inverse, split(reduced), NN))
                own[k] = next_high
                send_block(k)
                for b in range(members):
                    rows = slice(b * columns, (b + 1) * columns)
                    high[b, pl.ds(after, columns), at] = next_high[rows]
                    low[b, pl.ds(after, columns), at] = next_low[rows]

        return carry

    lax.fori_loop(0, BLOCKS + 1, turn, 0)

    for b in range(members):
        x = aug[b] * (steps_ref[b, 0] / 2.0**SQUARINGS)
        xs = split(x)
        x2 = product(xs, xs, NN)
        x2s = split(x2)
        x3 = product(xs, x2s, NN)
        x4 = product(x2s, x2s, NN)
        tail = x / 120.0 + x2 / 720.0 + x3 / 5040.0 + x4 / 40320.0
        aug[b] = x + x2 / 2.0 + x3 / 6.0 + x4 / 24.0 + product(split(x4), split(tail), NN)

    def square(index, carry):
        for b in range(members):
            now = aug[b]
            pair = split(now)
            aug[b] = 2.0 * now + product(pair, pair, NN)
        return carry

    lax.fori_loop(0, SQUARINGS - 1, square, 0)
    for b in range(members):
        now = aug[b]
        top = now[:columns]
        phi = 2.0 * top + product(split(top), split(now), NN)
        out_ref[b] = states_ref[b] + product(split(phi), (high[b], low[b]), NN)


def local(nr, nc, states, jacobian, step_sizes):
    members, columns, length = states.shape
    stacked = members * columns
    assert nr == nc == 2
    width = -(-(BLOCKS + 1) * columns // LANES) * LANES
    vmem = pl.BlockSpec(memory_space=pltpu.VMEM)
    dma = pltpu.SemaphoreType.DMA
    return pl.pallas_call(
        functools.partial(kernel, nr, nc),
        out_shape=jax.ShapeDtypeStruct(states.shape, f32),
        in_specs=[vmem, pl.BlockSpec(memory_space=pl.ANY), pl.BlockSpec(memory_space=pltpu.SMEM)],
        out_specs=vmem,
        scratch_shapes=[
            pltpu.VMEM(jacobian.shape, bf16),
            pltpu.VMEM((CHUNKS, stacked, length // CHUNKS), bf16),
            pltpu.VMEM((nr, CHUNKS, stacked, length // CHUNKS), bf16),
            pltpu.VMEM((stacked, length), f32),
            pltpu.VMEM((stacked, length), f32),
            pltpu.VMEM((members, width, length), bf16),
            pltpu.VMEM((members, width, length), bf16),
            pltpu.VMEM((stacked, length), f32),
            pltpu.VMEM((2, nr * nc, width // LANES, stacked, LANES), f32),
            pltpu.VMEM((members, width, width), f32),
            dma, dma((nr, CHUNKS)), dma((nc, CHUNKS)), dma, dma,
            dma((nr * nc - 1, width // LANES)), dma((2, nr * nc, width // LANES)),
        ],
        compiler_params=pltpu.CompilerParams(
            collective_id=0, has_side_effects=True, vmem_limit_bytes=48 * 2**20
        ),
    )(states, jacobian, step_sizes)


def solution(mesh):
    placed = (P("ens", None, ("row", "col")), P(("ens", "row"), "col"), P("ens", None))
    return jax.shard_map(
        functools.partial(local, mesh.shape["row"], mesh.shape["col"]), mesh=mesh,
        in_specs=placed, out_specs=P("ens", None, ("row", "col")), check_vma=False,
    )
```

```python
import functools

import jax
import jax.numpy as jnp
from jax import lax
from jax.experimental import pallas as pl
from jax.experimental.pallas import tpu as pltpu
from jax.sharding import PartitionSpec as P

BLOCKS = 12
SQUARINGS = 10
CHUNKS = 4
GROUP = 8
LANES = 128
MESH = pl.DeviceIdType.MESH
NN = (((1,), (0,)), ((), ()))
NT = (((1,), (1,)), ((), ()))
f32, bf16 = jnp.float32, jnp.bfloat16


def split(value):
    high = value.astype(bf16)
    return high, (value - high.astype(f32)).astype(bf16)


def product(left, right, dims):
    rows = left[0].shape[0]
    both = jnp.concatenate(left, axis=0)
    wide = lax.dot_general(both, right[0], dims, preferred_element_type=f32)
    low = lax.dot_general(left[0], right[1], dims, preferred_element_type=f32)
    return wide[:rows] + (wide[rows:] + low)


def factor(gram, place, offset):
    columns = gram.shape[0]
    lanes_inv = lax.broadcasted_iota(jnp.int32, (columns, place[1]), 1)
    diagonal = lax.broadcasted_iota(jnp.int32, (columns, place[1]), 0) + place[0]
    inverse = jnp.where(lanes_inv == diagonal, 1.0, 0.0).astype(f32)
    lanes = lax.broadcasted_iota(jnp.int32, (columns, offset[1]), 1)
    lower = jnp.zeros((columns, offset[1]), f32)
    sub = lax.broadcasted_iota(jnp.int32, (columns, LANES), 0)
    sub_inv = lax.broadcasted_iota(jnp.int32, (columns, place[1]), 0)
    for base in range(0, columns, GROUP):
        held = [
            jnp.broadcast_to(gram[:, base + i : base + i + 1], (columns, LANES))
            for i in range(GROUP)
        ]
        for i in range(GROUP):
            k = base + i
            pivot = held[i][k : k + 1, :]
            root = lax.rsqrt(pivot)
            root = root * (1.5 - 0.5 * pivot * root * root)
            column = jnp.where(sub >= k, held[i] * root, 0.0)
            below = jnp.where(sub > k, column, 0.0)
            for later in range(i + 1, GROUP):
                index = base + later
                held[later] = held[later] - below * column[index : index + 1, :]
            wide = jnp.concatenate([column] * (offset[1] // LANES), axis=1)
            lower = jnp.where(lanes == offset[0] + k, wide, lower)
            row = gram[k : k + 1, :] * root[:, :columns]
            row_inv = inverse[k : k + 1, :] * root[:, : place[1]]
            gram = gram - below[:, :columns] * row
            inverse = jnp.where(sub_inv == k, row_inv, inverse - below[:, : place[1]] * row_inv)
    return inverse, lower


def kernel(
    nr, nc, states_ref, jac_hbm, steps_ref, out_ref,
    jac, own, gathered, part_send, part_recv, high, low, w_ref, sums, aug,
    jac_sem, g_send, g_recv, p_send, p_recv, s_send, s_recv,
):
    members, columns, length = states_ref.shape
    stacked = members * columns
    width = high.shape[1]
    tiles = width // LANES
    chunk = length // CHUNKS
    r, c = lax.axis_index("row"), lax.axis_index("col")
    me = r * nc + c
    count = nr * nc

    load = pltpu.make_async_copy(jac_hbm, jac, jac_sem)
    load.start()
    barrier = pltpu.get_barrier_semaphore()
    for step in range(1, count):
        peer = lax.rem(me + step, count)
        pl.semaphore_signal(
            barrier, inc=1, device_id={"row": peer // nc, "col": lax.rem(peer, nc)},
            device_id_type=MESH,
        )
    high[...] = jnp.zeros_like(high)
    low[...] = jnp.zeros_like(low)
    aug[...] = jnp.zeros_like(aug)
    sums[...] = jnp.zeros_like(sums)
    pl.semaphore_wait(barrier, count - 1)

    to_self = c == r

    def block_copy(target, k):
        return pltpu.make_async_remote_copy(
            src_ref=own.at[k], dst_ref=gathered.at[c, k], send_sem=g_send.at[target, k],
            recv_sem=g_recv.at[c, k], device_id={"row": target, "col": r}, device_id_type=MESH,
        )

    def block_arrival(source, k):
        return pltpu.make_async_remote_copy(
            src_ref=own.at[k], dst_ref=gathered.at[source, k], send_sem=g_send.at[0, k],
            recv_sem=g_recv.at[source, k], device_id={"row": c, "col": source}, device_id_type=MESH,
        )

    def send_block(k):
        for target in range(nr):
            @pl.when(jnp.logical_not(jnp.logical_and(target == r, to_self)))
            def _():
                block_copy(target, k).start()

        @pl.when(to_self)
        def _():
            gathered[c, k] = own[k]

    def sum_copy(slot, step, i):
        peer = lax.rem(me + step, count)
        return pltpu.make_async_remote_copy(
            src_ref=sums.at[slot, me, i], dst_ref=sums.at[slot, me, i],
            send_sem=s_send.at[step - 1, i], recv_sem=s_recv.at[slot, me, i],
            device_id={"row": peer // nc, "col": lax.rem(peer, nc)}, device_id_type=MESH,
        )

    def sum_arrival(slot, step, i):
        peer = lax.rem(me + step, count)
        return pltpu.make_async_remote_copy(
            src_ref=sums.at[slot, peer, i], dst_ref=sums.at[slot, peer, i],
            send_sem=s_send.at[step - 1, i], recv_sem=s_recv.at[slot, peer, i],
            device_id={"row": peer // nc, "col": lax.rem(peer, nc)}, device_id_type=MESH,
        )

    def piece(owner, arrive):
        rows = pl.ds(pl.multiple_of(owner * length, length), length)
        total = None
        for k in range(CHUNKS):
            for source in range(nc):
                if arrive:
                    @pl.when(jnp.logical_not(jnp.logical_and(to_self, source == c)))
                    def _():
                        block_arrival(source, k).wait_recv()

                first = source * length + k * chunk
                term = lax.dot_general(
                    gathered[source, k], jac[rows, first : first + chunk], NT,
                    preferred_element_type=f32,
                )
                total = term if total is None else total + term
        return total

    for k in range(CHUNKS):
        own[k] = states_ref[...].reshape(stacked, length)[:, k * chunk : (k + 1) * chunk].astype(bf16)
        send_block(k)

    def turn(t, carry):
        @pl.when(t == 0)
        def _():
            load.wait()

        other = 1 - c
        part_send[...] = piece(other, True)
        partial = pltpu.make_async_remote_copy(
            src_ref=part_send, dst_ref=part_recv, send_sem=p_send, recv_sem=p_recv,
            device_id={"row": r, "col": other}, device_id_type=MESH,
        )
        partial.start()
        w_ref[...] = piece(c, False)
        for k in range(CHUNKS):
            for target in range(nr):
                @pl.when(jnp.logical_not(jnp.logical_and(target == r, to_self)))
                def _():
                    block_copy(target, k).wait_send()
        partial.wait()
        w_ref[...] = w_ref[...] + part_recv[...]

        @pl.when(t == 0)
        def _():
            first = states_ref[...].reshape(stacked, length)
            w_ref[...] = w_ref[...] - first * first * first / 3.0

        slot = lax.rem(t, 2)
        halves = []
        for b in range(members):
            w_high, w_low = split(w_ref[b * columns : (b + 1) * columns, :])
            high[b, :columns, :] = w_high
            low[b, :columns, :] = w_low
            halves.append((w_high, w_low))

        def project(i):
            at = slice(i * LANES, (i + 1) * LANES)
            for b in range(members):
                sums[slot, me, i, b * columns : (b + 1) * columns, :] = product(
                    halves[b], (high[b, at], low[b, at]), NT
                )
            for step in range(1, count):
                sum_copy(slot, step, i).start()

        def collect(i):
            for step in range(1, count):
                sum_arrival(slot, step, i).wait_recv()
            for step in range(1, count):
                sum_copy(slot, step, i).wait_send()

        project(0)
        for i in range(1, tiles):
            pl.when((t + 1) * columns > i * LANES)(functools.partial(project, i))
        collect(0)
        for i in range(1, tiles):
            pl.when((t + 1) * columns > i * LANES)(functools.partial(collect, i))
        parts = []
        for i in range(tiles):
            part = sums[slot, 0, i]
            for index in range(1, count):
                part = part + sums[slot, index, i]
            parts.append(part)
        total = jnp.concatenate(parts, axis=1)

        lanes = lax.broadcasted_iota(jnp.int32, (stacked, width), 1)
        projection = jnp.where(lanes >= columns, total, 0.0)
        start = pl.multiple_of(t * columns, columns)

        @pl.when(t == BLOCKS)
        def _():
            for b in range(members):
                aug[b, pl.ds(start, columns), :] = projection[b * columns : (b + 1) * columns]

        @pl.when(t < BLOCKS)
        def _():
            inverses, pairs = [], []
            for b in range(members):
                rows = slice(b * columns, (b + 1) * columns)
                term = projection[rows]
                pair = split(term)
                gram = total[rows, :columns] - product(pair, pair, NT)
                inverse, lower = factor(
                    gram, (b * columns, stacked), ((t + 1) * columns, width)
                )
                aug[b, pl.ds(start, columns), :] = term + lower
                inverses.append(inverse)
                pairs.append(pair)
            inverse = split(jnp.concatenate(inverses, axis=0))
            after = pl.multiple_of((t + 1) * columns, columns)
            for k in range(CHUNKS):
                at = slice(k * chunk, (k + 1) * chunk)
                reduced = jnp.concatenate(
                    [
                        w_ref[b * columns : (b + 1) * columns, at]
                        - product(pairs[b], (high[b, :, at], low[b, :, at]), NN)
                        for b in range(members)
                    ],
                    axis=0,
                )
                next_high, next_low = split(product(inverse, split(reduced), NN))
                own[k] = next_high
                send_block(k)
                for b in range(members):
                    rows = slice(b * columns, (b + 1) * columns)
                    high[b, pl.ds(after, columns), at] = next_high[rows]
                    low[b, pl.ds(after, columns), at] = next_low[rows]

        return carry

    lax.fori_loop(0, BLOCKS + 1, turn, 0)

    for b in range(members):
        x = aug[b] * (steps_ref[b, 0] / 2.0**SQUARINGS)
        xs = split(x)
        x2 = product(xs, xs, NN)
        x2s = split(x2)
        x3 = product(xs, x2s, NN)
        x4 = product(x2s, x2s, NN)
        tail = x / 120.0 + x2 / 720.0 + x3 / 5040.0 + x4 / 40320.0
        aug[b] = x + x2 / 2.0 + x3 / 6.0 + x4 / 24.0 + product(split(x4), split(tail), NN)

    def square(index, carry):
        for b in range(members):
            now = aug[b]
            pair = split(now)
            aug[b] = 2.0 * now + product(pair, pair, NN)
        return carry

    lax.fori_loop(0, SQUARINGS - 1, square, 0)
    for b in range(members):
        now = aug[b]
        top = now[:columns]
        phi = 2.0 * top + product(split(top), split(now), NN)
        out_ref[b] = states_ref[b] + product(split(phi), (high[b], low[b]), NN)


def local(nr, nc, states, jacobian, step_sizes):
    members, columns, length = states.shape
    stacked = members * columns
    assert nr == nc == 2
    width = -(-(BLOCKS + 1) * columns // LANES) * LANES
    vmem = pl.BlockSpec(memory_space=pltpu.VMEM)
    dma = pltpu.SemaphoreType.DMA
    return pl.pallas_call(
        functools.partial(kernel, nr, nc),
        out_shape=jax.ShapeDtypeStruct(states.shape, f32),
        in_specs=[vmem, pl.BlockSpec(memory_space=pl.ANY), pl.BlockSpec(memory_space=pltpu.SMEM)],
        out_specs=vmem,
        scratch_shapes=[
            pltpu.VMEM(jacobian.shape, bf16),
            pltpu.VMEM((CHUNKS, stacked, length // CHUNKS), bf16),
            pltpu.VMEM((nr, CHUNKS, stacked, length // CHUNKS), bf16),
            pltpu.VMEM((stacked, length), f32),
            pltpu.VMEM((stacked, length), f32),
            pltpu.VMEM((members, width, length), bf16),
            pltpu.VMEM((members, width, length), bf16),
            pltpu.VMEM((stacked, length), f32),
            pltpu.VMEM((2, nr * nc, width // LANES, stacked, LANES), f32),
            pltpu.VMEM((members, width, width), f32),
            dma, dma((nr, CHUNKS)), dma((nc, CHUNKS)), dma, dma,
            dma((nr * nc - 1, width // LANES)), dma((2, nr * nc, width // LANES)),
        ],
        compiler_params=pltpu.CompilerParams(
            collective_id=0, has_side_effects=True, vmem_limit_bytes=48 * 2**20
        ),
    )(states, jacobian, step_sizes)


def solution(mesh):
    placed = (P("ens", None, ("row", "col")), P(("ens", "row"), "col"), P("ens", None))
    return jax.shard_map(
        functools.partial(local, mesh.shape["row"], mesh.shape["col"]), mesh=mesh,
        in_specs=placed, out_specs=P("ens", None, ("row", "col")), check_vma=False,
    )
```

```python
import functools

import jax
import jax.numpy as jnp
from jax import lax
from jax.experimental import pallas as pl
from jax.experimental.pallas import tpu as pltpu
from jax.sharding import PartitionSpec as P

BLOCKS = 12
SQUARINGS = 10
CHUNKS = 4
GROUP = 16
LANES = 128
MESH = pl.DeviceIdType.MESH
NN = (((1,), (0,)), ((), ()))
NT = (((1,), (1,)), ((), ()))
f32, bf16 = jnp.float32, jnp.bfloat16


def split(value):
    high = value.astype(bf16)
    return high, (value - high.astype(f32)).astype(bf16)


def product(left, right, dims):
    rows = left[0].shape[0]
    both = jnp.concatenate(left, axis=0)
    wide = lax.dot_general(both, right[0], dims, preferred_element_type=f32)
    low = lax.dot_general(left[0], right[1], dims, preferred_element_type=f32)
    return wide[:rows] + (wide[rows:] + low)


def factor(gram, place, offset):
    columns = gram.shape[0]
    lanes_inv = lax.broadcasted_iota(jnp.int32, (columns, place[1]), 1)
    diagonal = lax.broadcasted_iota(jnp.int32, (columns, place[1]), 0) + place[0]
    inverse = jnp.where(lanes_inv == diagonal, 1.0, 0.0).astype(f32)
    lanes = lax.broadcasted_iota(jnp.int32, (columns, offset[1]), 1)
    lower = jnp.zeros((columns, offset[1]), f32)
    sub = lax.broadcasted_iota(jnp.int32, (columns, LANES), 0)
    sub_inv = lax.broadcasted_iota(jnp.int32, (columns, place[1]), 0)
    for base in range(0, columns, GROUP):
        held = [
            jnp.broadcast_to(gram[:, base + i : base + i + 1], (columns, LANES))
            for i in range(GROUP)
        ]
        for i in range(GROUP):
            k = base + i
            pivot = held[i][k : k + 1, :]
            root = lax.rsqrt(pivot)
            root = root * (1.5 - 0.5 * pivot * root * root)
            column = jnp.where(sub >= k, held[i] * root, 0.0)
            below = jnp.where(sub > k, column, 0.0)
            for later in range(i + 1, GROUP):
                index = base + later
                held[later] = held[later] - below * column[index : index + 1, :]
            wide = jnp.concatenate([column] * (offset[1] // LANES), axis=1)
            lower = jnp.where(lanes == offset[0] + k, wide, lower)
            row = gram[k : k + 1, :] * root[:, :columns]
            row_inv = inverse[k : k + 1, :] * root[:, : place[1]]
            gram = gram - below[:, :columns] * row
            inverse = jnp.where(sub_inv == k, row_inv, inverse - below[:, : place[1]] * row_inv)
    return inverse, lower


def kernel(
    nr, nc, states_ref, jac_hbm, steps_ref, out_ref,
    jac, own, gathered, part_send, part_recv, high, low, w_ref, sums, aug,
    jac_sem, g_send, g_recv, p_send, p_recv, s_send, s_recv,
):
    members, columns, length = states_ref.shape
    stacked = members * columns
    width = high.shape[1]
    tiles = width // LANES
    chunk = length // CHUNKS
    r, c = lax.axis_index("row"), lax.axis_index("col")
    me = r * nc + c
    count = nr * nc

    load = pltpu.make_async_copy(jac_hbm, jac, jac_sem)
    load.start()
    barrier = pltpu.get_barrier_semaphore()
    for step in range(1, count):
        peer = lax.rem(me + step, count)
        pl.semaphore_signal(
            barrier, inc=1, device_id={"row": peer // nc, "col": lax.rem(peer, nc)},
            device_id_type=MESH,
        )
    high[...] = jnp.zeros_like(high)
    low[...] = jnp.zeros_like(low)
    aug[...] = jnp.zeros_like(aug)
    sums[...] = jnp.zeros_like(sums)
    pl.semaphore_wait(barrier, count - 1)

    to_self = c == r

    def block_copy(target, k):
        return pltpu.make_async_remote_copy(
            src_ref=own.at[k], dst_ref=gathered.at[c, k], send_sem=g_send.at[target, k],
            recv_sem=g_recv.at[c, k], device_id={"row": target, "col": r}, device_id_type=MESH,
        )

    def block_arrival(source, k):
        return pltpu.make_async_remote_copy(
            src_ref=own.at[k], dst_ref=gathered.at[source, k], send_sem=g_send.at[0, k],
            recv_sem=g_recv.at[source, k], device_id={"row": c, "col": source}, device_id_type=MESH,
        )

    def send_block(k):
        for target in range(nr):
            @pl.when(jnp.logical_not(jnp.logical_and(target == r, to_self)))
            def _():
                block_copy(target, k).start()

        @pl.when(to_self)
        def _():
            gathered[c, k] = own[k]

    def sum_copy(slot, step, i):
        peer = lax.rem(me + step, count)
        return pltpu.make_async_remote_copy(
            src_ref=sums.at[slot, me, i], dst_ref=sums.at[slot, me, i],
            send_sem=s_send.at[step - 1, i], recv_sem=s_recv.at[slot, me, i],
            device_id={"row": peer // nc, "col": lax.rem(peer, nc)}, device_id_type=MESH,
        )

    def sum_arrival(slot, step, i):
        peer = lax.rem(me + step, count)
        return pltpu.make_async_remote_copy(
            src_ref=sums.at[slot, peer, i], dst_ref=sums.at[slot, peer, i],
            send_sem=s_send.at[step - 1, i], recv_sem=s_recv.at[slot, peer, i],
            device_id={"row": peer // nc, "col": lax.rem(peer, nc)}, device_id_type=MESH,
        )

    def piece(owner, arrive):
        rows = pl.ds(pl.multiple_of(owner * length, length), length)
        total = None
        for k in range(CHUNKS):
            for source in range(nc):
                if arrive:
                    @pl.when(jnp.logical_not(jnp.logical_and(to_self, source == c)))
                    def _():
                        block_arrival(source, k).wait_recv()

                first = source * length + k * chunk
                term = lax.dot_general(
                    gathered[source, k], jac[rows, first : first + chunk], NT,
                    preferred_element_type=f32,
                )
                total = term if total is None else total + term
        return total

    for k in range(CHUNKS):
        own[k] = states_ref[...].reshape(stacked, length)[:, k * chunk : (k + 1) * chunk].astype(bf16)
        send_block(k)

    def turn(t, carry):
        @pl.when(t == 0)
        def _():
            load.wait()

        other = 1 - c
        part_send[...] = piece(other, True)
        partial = pltpu.make_async_remote_copy(
            src_ref=part_send, dst_ref=part_recv, send_sem=p_send, recv_sem=p_recv,
            device_id={"row": r, "col": other}, device_id_type=MESH,
        )
        partial.start()
        w_ref[...] = piece(c, False)
        for k in range(CHUNKS):
            for target in range(nr):
                @pl.when(jnp.logical_not(jnp.logical_and(target == r, to_self)))
                def _():
                    block_copy(target, k).wait_send()
        partial.wait()
        w_ref[...] = w_ref[...] + part_recv[...]

        @pl.when(t == 0)
        def _():
            first = states_ref[...].reshape(stacked, length)
            w_ref[...] = w_ref[...] - first * first * first / 3.0

        slot = lax.rem(t, 2)
        halves = []
        for b in range(members):
            w_high, w_low = split(w_ref[b * columns : (b + 1) * columns, :])
            high[b, :columns, :] = w_high
            low[b, :columns, :] = w_low
            halves.append((w_high, w_low))

        def project(i):
            at = slice(i * LANES, (i + 1) * LANES)
            for b in range(members):
                sums[slot, me, i, b * columns : (b + 1) * columns, :] = product(
                    halves[b], (high[b, at], low[b, at]), NT
                )
            for step in range(1, count):
                sum_copy(slot, step, i).start()

        def collect(i):
            for step in range(1, count):
                sum_arrival(slot, step, i).wait_recv()
            for step in range(1, count):
                sum_copy(slot, step, i).wait_send()

        project(0)
        for i in range(1, tiles):
            pl.when((t + 1) * columns > i * LANES)(functools.partial(project, i))
        collect(0)
        for i in range(1, tiles):
            pl.when((t + 1) * columns > i * LANES)(functools.partial(collect, i))
        parts = []
        for i in range(tiles):
            part = sums[slot, 0, i]
            for index in range(1, count):
                part = part + sums[slot, index, i]
            parts.append(part)
        total = jnp.concatenate(parts, axis=1)

        lanes = lax.broadcasted_iota(jnp.int32, (stacked, width), 1)
        projection = jnp.where(lanes >= columns, total, 0.0)
        start = pl.multiple_of(t * columns, columns)

        @pl.when(t == BLOCKS)
        def _():
            for b in range(members):
                aug[b, pl.ds(start, columns), :] = projection[b * columns : (b + 1) * columns]

        @pl.when(t < BLOCKS)
        def _():
            inverses, pairs = [], []
            for b in range(members):
                rows = slice(b * columns, (b + 1) * columns)
                term = projection[rows]
                pair = split(term)
                gram = total[rows, :columns] - product(pair, pair, NT)
                inverse, lower = factor(
                    gram, (b * columns, stacked), ((t + 1) * columns, width)
                )
                aug[b, pl.ds(start, columns), :] = term + lower
                inverses.append(inverse)
                pairs.append(pair)
            inverse = split(jnp.concatenate(inverses, axis=0))
            after = pl.multiple_of((t + 1) * columns, columns)
            for k in range(CHUNKS):
                at = slice(k * chunk, (k + 1) * chunk)
                reduced = jnp.concatenate(
                    [
                        w_ref[b * columns : (b + 1) * columns, at]
                        - product(pairs[b], (high[b, :, at], low[b, :, at]), NN)
                        for b in range(members)
                    ],
                    axis=0,
                )
                next_high, next_low = split(product(inverse, split(reduced), NN))
                own[k] = next_high
                send_block(k)
                for b in range(members):
                    rows = slice(b * columns, (b + 1) * columns)
                    high[b, pl.ds(after, columns), at] = next_high[rows]
                    low[b, pl.ds(after, columns), at] = next_low[rows]

        return carry

    lax.fori_loop(0, BLOCKS + 1, turn, 0)

    for b in range(members):
        x = aug[b] * (steps_ref[b, 0] / 2.0**SQUARINGS)
        xs = split(x)
        x2 = product(xs, xs, NN)
        x2s = split(x2)
        x3 = product(xs, x2s, NN)
        x4 = product(x2s, x2s, NN)
        tail = x / 120.0 + x2 / 720.0 + x3 / 5040.0 + x4 / 40320.0
        aug[b] = x + x2 / 2.0 + x3 / 6.0 + x4 / 24.0 + product(split(x4), split(tail), NN)

    def square(index, carry):
        for b in range(members):
            now = aug[b]
            pair = split(now)
            aug[b] = 2.0 * now + product(pair, pair, NN)
        return carry

    lax.fori_loop(0, SQUARINGS - 1, square, 0)
    for b in range(members):
        now = aug[b]
        top = now[:columns]
        phi = 2.0 * top + product(split(top), split(now), NN)
        out_ref[b] = states_ref[b] + product(split(phi), (high[b], low[b]), NN)


def local(nr, nc, states, jacobian, step_sizes):
    members, columns, length = states.shape
    stacked = members * columns
    assert nr == nc == 2
    width = -(-(BLOCKS + 1) * columns // LANES) * LANES
    vmem = pl.BlockSpec(memory_space=pltpu.VMEM)
    dma = pltpu.SemaphoreType.DMA
    return pl.pallas_call(
        functools.partial(kernel, nr, nc),
        out_shape=jax.ShapeDtypeStruct(states.shape, f32),
        in_specs=[vmem, pl.BlockSpec(memory_space=pl.ANY), pl.BlockSpec(memory_space=pltpu.SMEM)],
        out_specs=vmem,
        scratch_shapes=[
            pltpu.VMEM(jacobian.shape, bf16),
            pltpu.VMEM((CHUNKS, stacked, length // CHUNKS), bf16),
            pltpu.VMEM((nr, CHUNKS, stacked, length // CHUNKS), bf16),
            pltpu.VMEM((stacked, length), f32),
            pltpu.VMEM((stacked, length), f32),
            pltpu.VMEM((members, width, length), bf16),
            pltpu.VMEM((members, width, length), bf16),
            pltpu.VMEM((stacked, length), f32),
            pltpu.VMEM((2, nr * nc, width // LANES, stacked, LANES), f32),
            pltpu.VMEM((members, width, width), f32),
            dma, dma((nr, CHUNKS)), dma((nc, CHUNKS)), dma, dma,
            dma((nr * nc - 1, width // LANES)), dma((2, nr * nc, width // LANES)),
        ],
        compiler_params=pltpu.CompilerParams(
            collective_id=0, has_side_effects=True, vmem_limit_bytes=48 * 2**20
        ),
    )(states, jacobian, step_sizes)


def solution(mesh):
    placed = (P("ens", None, ("row", "col")), P(("ens", "row"), "col"), P("ens", None))
    return jax.shard_map(
        functools.partial(local, mesh.shape["row"], mesh.shape["col"]), mesh=mesh,
        in_specs=placed, out_specs=P("ens", None, ("row", "col")), check_vma=False,
    )
```
